32 devices in a mesh: row: 8 (over z, x), col: 4 (over y, core).
Axes of the slice: x: 2, y: 2, z: 4, core: 2. Of those that a mesh axis runs over, the one named last changes fastest.
Arguments:
- affinity: bfloat16 [32768, 8192], P('row', 'col'), may hold values from -250 to 250
- seed_values: int32 [16], replicated, may hold values from 0 to 1073741823
- sku_ids: int32 [8192], P('col'), may hold values from 0 to 8191, each once
Outputs:
- range_basis: float32 [16, 32768], P(None, ('row', 'col'))
- range_factor: float32 [16, 16], replicated
The draws below stay inside these ranges and needn't reach their ends.
All inputs are finite; a program needn't handle non-finite values.
Results may differ from the reference program's by a relative error of at most 0.0046.
Values may be sent and summed in bfloat16 or wider, within the bound.
A program may use at most 64 MiB of HBM per device.

```python
import math
import jax
import jax.numpy as jnp
from jax import lax

N = 8192
K = 16
ITERS = 2
ROWS = 32768


def draw_affinity(key, part):
    key_base = jax.random.fold_in(key, 11)
    key_rows = jax.random.fold_in(key, 12)
    key_cols = jax.random.fold_in(key, 13)
    position = jnp.arange(ROWS, dtype=jnp.float32)[:, None] / ROWS
    base = jax.random.normal(key_base, (ROWS, N), jnp.float32)
    trend = jnp.exp(math.log(3.0) * position)
    row_scale = jnp.exp(jax.random.uniform(key_rows, (ROWS, 1), jnp.float32, math.log(0.3), math.log(3.0)))
    col_scale = jnp.exp(jax.random.uniform(key_cols, (1, N), jnp.float32, math.log(0.5), math.log(2.0)))
    return (base * trend * row_scale * col_scale).astype(jnp.bfloat16)


def place_ends(result, key, smallest, top_value):
    place = [jax.random.randint(jax.random.fold_in(key, axis), (), 0, length) for axis, length in enumerate(result.shape)]
    longest = result.shape.index(max(result.shape))
    neighbour = place[:longest] + [(place[longest] + 1) % result.shape[longest]] + place[longest + 1:]
    return result.at[tuple(place)].set(smallest).at[tuple(neighbour)].set(top_value)


def setup_inputs(seed: int = 0) -> dict:
    keys = jax.random.split(jax.random.key(seed), 4)
    return {
        "affinity": draw_affinity(jax.random.fold_in(keys[3], 71), 0),
        "seed_values": place_ends(jax.random.randint(keys[1], (K,), 0, 1073741824), jax.random.fold_in(keys[1], 1), 0, 1073741823).astype(jnp.int32),
        "sku_ids": jax.random.permutation(keys[2], N).astype(jnp.int32),
    }


mix_first = -2048144789
mix_second = -1028477387
golden = -1640531535
salt_value = 1540483477

def shifted(value, amount):
    return lax.shift_right_logical(value, jnp.full(value.shape, amount, jnp.int32))

def scramble(value):
    value = jnp.bitwise_xor(value, shifted(value, 16))
    value = value * jnp.int32(mix_first)
    value = jnp.bitwise_xor(value, shifted(value, 13))
    value = value * jnp.int32(mix_second)
    return jnp.bitwise_xor(value, shifted(value, 16))

def test_matrix(seed_values, sku_ids, total_columns):
    first = scramble(jnp.bitwise_xor(seed_values[:, None], sku_ids[None, :] * jnp.int32(golden)))
    second = scramble(jnp.bitwise_xor(first, jnp.int32(salt_value)))
    uniform_a = (shifted(first, 9) + 1).astype(jnp.float32) / 8388608.0
    uniform_b = (shifted(second, 9) + 1).astype(jnp.float32) / 8388608.0
    gauss = jnp.sqrt(-2.0 * jnp.log(uniform_a)) * jnp.cos(6.283185307179586 * uniform_b)
    return (gauss / math.sqrt(total_columns)).astype(jnp.bfloat16)

def project(left, affinity):
    return lax.dot_general(left.astype(jnp.float32), affinity.astype(jnp.float32), (((1,), (1,)), ((), ())), preferred_element_type=jnp.float32)

def lower_solve(lower, right):
    return lax.linalg.triangular_solve(lower, right, left_side=True, lower=True)

def reference(affinity, seed_values, sku_ids):
    omega = test_matrix(seed_values, sku_ids, N)
    sketch = project(omega, affinity)
    for repeat in range(ITERS + 1):
        gram = jnp.dot(sketch.astype(jnp.float32), sketch.T.astype(jnp.float32), precision=lax.Precision.HIGHEST, preferred_element_type=jnp.float32)
        lower = jnp.linalg.cholesky(gram)
        ortho = lower_solve(lower, sketch)
        if repeat < ITERS:
            back = jnp.dot(ortho.astype(jnp.bfloat16).astype(jnp.float32), affinity.astype(jnp.float32), preferred_element_type=jnp.float32)
            sketch = project(back.astype(jnp.bfloat16), affinity) * (1.0 / math.sqrt(N))
    scale = math.sqrt(ROWS)
    return (ortho * scale, lower.T / scale)
```

```python
import functools
import math

import jax
import jax.numpy as jnp
from jax import lax
from jax.experimental import pallas as pl
from jax.experimental.pallas import tpu as pltpu
from jax.sharding import PartitionSpec as P

ITERS = 2
HIGHEST = lax.Precision.HIGHEST
MESH = pl.DeviceIdType.MESH

mix_first = -2048144789
mix_second = -1028477387
golden = -1640531535
salt_value = 1540483477


def shifted(value, amount):
    return lax.shift_right_logical(value, jnp.full(value.shape, amount, jnp.int32))


def scramble(value):
    value = jnp.bitwise_xor(value, shifted(value, 16))
    value = value * jnp.int32(mix_first)
    value = jnp.bitwise_xor(value, shifted(value, 13))
    value = value * jnp.int32(mix_second)
    return jnp.bitwise_xor(value, shifted(value, 16))


def test_matrix(seeds, skus, total_columns):
    first = scramble(jnp.bitwise_xor(seeds, skus * jnp.int32(golden)))
    second = scramble(jnp.bitwise_xor(first, jnp.int32(salt_value)))
    uniform_a = (shifted(first, 9) + 1).astype(jnp.float32) / 8388608.0
    uniform_b = (shifted(second, 9) + 1).astype(jnp.float32) / 8388608.0
    gauss = jnp.sqrt(-2.0 * jnp.log(uniform_a)) * jnp.cos(6.283185307179586 * uniform_b)
    return (gauss / math.sqrt(total_columns)).astype(jnp.bfloat16)


def factorize(gram):
    count = gram.shape[0]
    rows = lax.broadcasted_iota(jnp.int32, (count, count), 0)
    cols = lax.broadcasted_iota(jnp.int32, (count, count), 1)
    left = gram
    right = (rows == cols).astype(jnp.float32)
    for j in range(count):
        pivot = left[j : j + 1, j : j + 1]
        inv = lax.rsqrt(pivot)
        inv = inv * (1.5 - 0.5 * (pivot * inv) * inv)
        left_row = left[j : j + 1, :] * inv
        right_row = right[j : j + 1, :] * inv
        factor = left[:, j : j + 1] * inv
        left = jnp.where(rows == j, left_row, jnp.where(rows > j, left - factor * left_row, left))
        right = jnp.where(rows == j, right_row, jnp.where(rows > j, right - factor * right_row, right))
    return jnp.where(rows <= cols, left, 0.0), right


def kernel(
    dims,
    slab_hbm, seed_ref, sku_ref,
    basis_ref, factor_ref,
    slab, x_ref, part, sum_recv, s_ref, lhs, zacc, zpart, zrecv, back, gsend_row, grecv_row, grecv_col, gcol,
    load_sem, sum_send_sem, sum_recv_sem, s_send_sem, s_recv_sem,
    z_send_sem, z_recv_sem, b_send_sem, b_recv_sem, g_send_sem, g_recv_sem, c_send_sem, c_recv_sem,
):
    R, C, K, piece, width, inv_root, scale = dims
    w = width // R
    me_r = lax.axis_index("row")
    me_c = lax.axis_index("col")

    def col_peer(k):
        return lax.rem(me_c + k, C)

    def row_peer(k):
        return lax.rem(me_r + k, R)

    def col_from(k):
        return lax.rem(me_c + (C - k), C)

    def row_from(k):
        return lax.rem(me_r + (R - k), R)

    order = list(range(1, C)) + [0]

    def load(k):
        c = col_peer(k)
        return pltpu.make_async_copy(
            slab_hbm.at[pl.ds(pl.multiple_of(c * piece, piece), piece), :], slab.at[c], load_sem.at[k]
        )

    for k in order:
        load(k).start()

    barrier = pltpu.get_barrier_semaphore()
    for k in range(1, R):
        pl.semaphore_signal(barrier, inc=1, device_id={"row": row_peer(k)}, device_id_type=MESH)
    for k in range(1, C):
        pl.semaphore_signal(barrier, inc=1, device_id={"col": col_peer(k)}, device_id_type=MESH)

    index = lax.broadcasted_iota(jnp.int32, (K, width), 0)
    seeds = jnp.zeros((K, width), jnp.int32)
    for k in range(K):
        seeds = jnp.where(index == k, seed_ref[k], seeds)
    x_ref[...] = test_matrix(seeds, jnp.broadcast_to(sku_ref[...], (K, width)), width * C)

    pl.semaphore_wait(barrier, (R - 1) + (C - 1))

    pending = []

    def col_copy(src, dst, send, recv, k):
        return pltpu.make_async_remote_copy(
            src_ref=src, dst_ref=dst, send_sem=send, recv_sem=recv,
            device_id={"col": col_peer(k)}, device_id_type=MESH,
        )

    def row_copy(src, dst, send, recv, k):
        return pltpu.make_async_remote_copy(
            src_ref=src, dst_ref=dst, send_sem=send, recv_sem=recv,
            device_id={"row": row_peer(k)}, device_id_type=MESH,
        )

    def project(c):
        return lax.dot_general(
            x_ref[...], slab[c], (((1,), (1,)), ((), ())), preferred_element_type=jnp.float32
        )

    for it in range(ITERS + 1):
        copies = []
        for k in order:
            if it == 0:
                load(k).wait()
            c = col_peer(k)
            if k == 0:
                own = project(c)
            else:
                part[it, k] = project(c)
                copy = col_copy(
                    part.at[it, k], sum_recv.at[it, k], sum_send_sem.at[it, k], sum_recv_sem.at[it, k], k
                )
                copy.start()
                copies.append((k, copy))
        for k, copy in copies:
            copy.wait_recv()
            own = own + sum_recv[it, k]
            pending.append(copy)
        if it > 0:
            own = own * inv_root

        if it == ITERS:
            gram = lax.dot_general(
                own, own, (((1,), (1,)), ((), ())), precision=HIGHEST, preferred_element_type=jnp.float32
            )
            gcol[...] = gram
            copies = []
            for k in range(1, C):
                copy = col_copy(gcol, grecv_col.at[me_c], c_send_sem.at[k], c_recv_sem.at[k], k)
                copy.start()
                copies.append(copy)
            grecv_col[me_c] = gram
            for k in range(1, C):
                col_copy(
                    gcol, grecv_col.at[col_from(k)], c_send_sem.at[k], c_recv_sem.at[k], k
                ).wait_recv()
            pending += copies
            gram = grecv_col[0]
            for c in range(1, C):
                gram = gram + grecv_col[c]
        else:
            s_ref[it, me_c] = own
            for k in range(1, C):
                copy = col_copy(
                    s_ref.at[it, me_c], s_ref.at[it, me_c], s_send_sem.at[it, k], s_recv_sem.at[it, k], k
                )
                copy.start()
                pending.append(copy)
            gram = None
            for k in range(C):
                c = col_from(k)
                if k > 0:
                    col_copy(
                        s_ref.at[it, c], s_ref.at[it, c], s_send_sem.at[it, k], s_recv_sem.at[it, k], k
                    ).wait_recv()
                value = s_ref[it, c]
                high = value.astype(jnp.bfloat16)
                low = (value - high.astype(jnp.float32)).astype(jnp.bfloat16)
                lhs[:K, :] = high
                lhs[K:, :] = low
                if k < C - 1 or w % 128:
                    product = jnp.dot(lhs[...], slab[c], preferred_element_type=jnp.float32)
                    product = product[:K] + product[K:]
                    zacc[...] = product if k == 0 else zacc[...] + product
            for c in range(C):
                value = s_ref[it, c]
                term = lax.dot_general(
                    value, value, (((1,), (1,)), ((), ())), precision=HIGHEST, preferred_element_type=jnp.float32
                )
                gram = term if c == 0 else gram + term

        gsend_row[it] = gram
        for k in range(1, R):
            copy = row_copy(
                gsend_row.at[it], grecv_row.at[it, me_r], g_send_sem.at[it, k], g_recv_sem.at[it, k], k
            )
            copy.start()
            pending.append(copy)
        grecv_row[it, me_r] = gram

        if it < ITERS:
            last = col_from(C - 1)
            if w % 128:
                for r in range(R):
                    zpart[it, r] = zacc[:, r * w : (r + 1) * w]
            z_copies = []
            for k in list(range(1, R)) + [0]:
                r = row_peer(k)
                if w % 128 == 0:
                    span = pl.ds(pl.multiple_of(r * w, w), w)
                    product = jnp.dot(lhs[...], slab[last, :, span], preferred_element_type=jnp.float32)
                    zpart[it, r] = zacc[:, span] + product[:K] + product[K:]
                if k > 0:
                    copy = row_copy(
                        zpart.at[it, r], zrecv.at[it, k], z_send_sem.at[it, k], z_recv_sem.at[it, k], k
                    )
                    copy.start()
                    z_copies.append((k, copy))

        for k in range(1, R):
            row_copy(
                gsend_row.at[it], grecv_row.at[it, row_from(k)], g_send_sem.at[it, k], g_recv_sem.at[it, k], k
            ).wait_recv()
        gram = grecv_row[it, 0]
        for r in range(1, R):
            gram = gram + grecv_row[it, r]
        upper, inverse = factorize(gram)

        if it == ITERS:
            ortho = jnp.dot(inverse, own, precision=HIGHEST, preferred_element_type=jnp.float32)
            basis_ref[...] = ortho * scale
            factor_ref[...] = upper / scale
        else:
            total = zpart[it, me_r]
            for k, copy in z_copies:
                copy.wait_recv()
                total = total + zrecv[it, k]
                pending.append(copy)
            back[it, me_r] = jnp.dot(
                inverse, total, precision=HIGHEST, preferred_element_type=jnp.float32
            ).astype(jnp.bfloat16)
            for k in range(1, R):
                copy = row_copy(
                    back.at[it, me_r], back.at[it, me_r], b_send_sem.at[it, k], b_recv_sem.at[it, k], k
                )
                copy.start()
                pending.append(copy)
            for k in range(1, R):
                r = row_from(k)
                row_copy(
                    back.at[it, r], back.at[it, r], b_send_sem.at[it, k], b_recv_sem.at[it, k], k
                ).wait_recv()
            for r in range(R):
                x_ref[:, r * w : (r + 1) * w] = back[it, r]

    for copy in pending:
        copy.wait_send()


def body(affinity, seed_values, sku_ids):
    R, C = lax.axis_size("row"), lax.axis_size("col")
    K = seed_values.shape[0]
    rows, width = affinity.shape
    piece, w = rows // C, width // R
    dims = (R, C, K, piece, width, 1.0 / math.sqrt(width * C), math.sqrt(rows * R))
    f32, bf16 = jnp.float32, jnp.bfloat16
    dma = pltpu.SemaphoreType.DMA
    vmem = pl.BlockSpec(memory_space=pltpu.VMEM)
    return pl.pallas_call(
        functools.partial(kernel, dims),
        out_shape=(
            jax.ShapeDtypeStruct((K, piece), f32),
            jax.ShapeDtypeStruct((K, K), f32),
        ),
        in_specs=[
            pl.BlockSpec(memory_space=pl.ANY),
            pl.BlockSpec(memory_space=pltpu.SMEM),
            vmem,
        ],
        out_specs=(vmem, vmem),
        scratch_shapes=[
            pltpu.VMEM((C, piece, width), bf16),
            pltpu.VMEM((K, width), bf16),
            pltpu.VMEM((ITERS + 1, C, K, piece), f32),
            pltpu.VMEM((ITERS + 1, C, K, piece), f32),
            pltpu.VMEM((ITERS, C, K, piece), f32),
            pltpu.VMEM((2 * K, piece), bf16),
            pltpu.VMEM((K, width), f32),
            pltpu.VMEM((ITERS, R, K, w), f32),
            pltpu.VMEM((ITERS, R, K, w), f32),
            pltpu.VMEM((ITERS, R, K, w), bf16),
            pltpu.VMEM((ITERS + 1, K, K), f32),
            pltpu.VMEM((ITERS + 1, R, K, K), f32),
            pltpu.VMEM((C, K, K), f32),
            pltpu.VMEM((K, K), f32),
            dma((C,)),
            dma((ITERS + 1, C)), dma((ITERS + 1, C)),
            dma((ITERS, C)), dma((ITERS, C)),
            dma((ITERS, R)), dma((ITERS, R)),
            dma((ITERS, R)), dma((ITERS, R)),
            dma((ITERS + 1, R)), dma((ITERS + 1, R)),
            dma((C,)), dma((C,)),
        ],
        compiler_params=pltpu.CompilerParams(
            collective_id=0, has_side_effects=True, vmem_limit_bytes=60 * 1024 * 1024
        ),
    )(affinity, seed_values, sku_ids[None, :])


def solution(mesh):
    placed = (P("row", "col"), P(), P("col"))
    return jax.shard_map(
        body, mesh=mesh, in_specs=placed, out_specs=(P(None, ("row", "col")), P()), check_vma=False
    )
```

```python
import functools
import math

import jax
import jax.numpy as jnp
from jax import lax
from jax.experimental import pallas as pl
from jax.experimental.pallas import tpu as pltpu
from jax.sharding import PartitionSpec as P

ITERS = 2
HIGHEST = lax.Precision.HIGHEST
MESH = pl.DeviceIdType.MESH

mix_first = -2048144789
mix_second = -1028477387
golden = -1640531535
salt_value = 1540483477


def shifted(value, amount):
    return lax.shift_right_logical(value, jnp.full(value.shape, amount, jnp.int32))


def scramble(value):
    value = jnp.bitwise_xor(value, shifted(value, 16))
    value = value * jnp.int32(mix_first)
    value = jnp.bitwise_xor(value, shifted(value, 13))
    value = value * jnp.int32(mix_second)
    return jnp.bitwise_xor(value, shifted(value, 16))


def test_matrix(seeds, skus, total_columns):
    first = scramble(jnp.bitwise_xor(seeds, skus * jnp.int32(golden)))
    second = scramble(jnp.bitwise_xor(first, jnp.int32(salt_value)))
    uniform_a = (shifted(first, 9) + 1).astype(jnp.float32) / 8388608.0
    uniform_b = (shifted(second, 9) + 1).astype(jnp.float32) / 8388608.0
    gauss = jnp.sqrt(-2.0 * jnp.log(uniform_a)) * jnp.cos(6.283185307179586 * uniform_b)
    return (gauss / math.sqrt(total_columns)).astype(jnp.bfloat16)


def factorize(gram):
    count = gram.shape[0]
    rows = lax.broadcasted_iota(jnp.int32, (count, count), 0)
    cols = lax.broadcasted_iota(jnp.int32, (count, count), 1)
    left = gram
    right = (rows == cols).astype(jnp.float32)
    for j in range(count):
        pivot = left[j : j + 1, j : j + 1]
        inv = lax.rsqrt(pivot)
        inv = inv * (1.5 - 0.5 * (pivot * inv) * inv)
        left_row = left[j : j + 1, :] * inv
        right_row = right[j : j + 1, :] * inv
        factor = left[:, j : j + 1] * inv
        left = jnp.where(rows == j, left_row, jnp.where(rows > j, left - factor * left_row, left))
        right = jnp.where(rows == j, right_row, jnp.where(rows > j, right - factor * right_row, right))
    return jnp.where(rows <= cols, left, 0.0), right


def kernel(
    dims,
    slab_hbm, seed_ref, sku_ref,
    basis_ref, factor_ref,
    slab, slab_t, x_ref, part, half_recv, y_sum, part_last, recv_last, s_ref, lhs, zacc, zpart, zrecv, back,
    gsend_row, grecv_row, grecv_col, gcol, gram_part,
    load_sem, a_send_sem, a_recv_sem, y_send_sem, y_recv_sem, last_send_sem, last_recv_sem, s_send_sem, s_recv_sem,
    z_send_sem, z_recv_sem, b_send_sem, b_recv_sem, g_send_sem, g_recv_sem, c_send_sem, c_recv_sem,
):
    R, C, K, piece, width, inv_root, scale = dims
    w = width // R
    me_r = lax.axis_index("row")
    me_c = lax.axis_index("col")

    Y = C // 2
    core, me_y = lax.rem(me_c, 2), me_c // 2
    partner = me_y * 2 + (1 - core)

    def y_peer(k):
        return lax.rem(me_y + k, Y) * 2 + core

    def col_peer_of(k):
        return (1 - core) * Y + k if k < Y else core * Y + k - Y

    def row_peer(k):
        return lax.rem(me_r + k, R)

    def row_from(k):
        return lax.rem(me_r + (R - k), R)

    def load(k):
        c = col_peer_of(k)
        return pltpu.make_async_copy(
            slab_hbm.at[pl.ds(pl.multiple_of(c * piece, piece), piece), :], slab.at[c], load_sem.at[k]
        )

    for k in range(C):
        load(k).start()

    barrier = pltpu.get_barrier_semaphore()
    for k in range(1, R):
        pl.semaphore_signal(barrier, inc=1, device_id={"row": row_peer(k)}, device_id_type=MESH)
    for k in range(1, C):
        pl.semaphore_signal(barrier, inc=1, device_id={"col": lax.rem(me_c + k, C)}, device_id_type=MESH)

    index = lax.broadcasted_iota(jnp.int32, (K, width), 0)
    seeds = jnp.zeros((K, width), jnp.int32)
    for k in range(K):
        seeds = jnp.where(index == k, seed_ref[k], seeds)
    x_ref[...] = test_matrix(seeds, jnp.broadcast_to(sku_ref[...], (K, width)), width * C)

    pl.semaphore_wait(barrier, (R - 1) + (C - 1))

    pending = []

    def col_copy(src, dst, send, recv, target):
        return pltpu.make_async_remote_copy(
            src_ref=src, dst_ref=dst, send_sem=send, recv_sem=recv,
            device_id={"col": lax.rem(target, C)}, device_id_type=MESH,
        )

    def row_copy(src, dst, send, recv, k):
        return pltpu.make_async_remote_copy(
            src_ref=src, dst_ref=dst, send_sem=send, recv_sem=recv,
            device_id={"row": row_peer(k)}, device_id_type=MESH,
        )

    def project(c):
        return jnp.dot(x_ref[...], slab_t[c], preferred_element_type=jnp.float32)

    def fetch(k):
        load(k).wait()
        c = col_peer_of(k)
        slab_t[c] = slab[c].T

    def square(value):
        return lax.dot_general(
            value, value, (((1,), (1,)), ((), ())), precision=HIGHEST, preferred_element_type=jnp.float32
        )

    for it in range(ITERS + 1):
        if it == ITERS:
            copies = []
            for k in list(range(1, C)) + [0]:
                c = lax.rem(me_c + k, C)
                if k == 0:
                    own = project(c)
                else:
                    part_last[k] = project(c)
                    copy = col_copy(
                        part_last.at[k], recv_last.at[k], last_send_sem.at[k], last_recv_sem.at[k], me_c + k
                    )
                    copy.start()
                    copies.append(copy)
            for k, copy in enumerate(copies):
                copy.wait_recv()
                own = own + recv_last[k + 1]
            pending += copies
            own = own * inv_root
            gram = square(own)
            gcol[...] = gram
            copies = []
            for k in range(1, C):
                copy = col_copy(gcol, grecv_col.at[me_c], c_send_sem.at[k], c_recv_sem.at[k], me_c + k)
                copy.start()
                copies.append(copy)
            grecv_col[me_c] = gram
            for k in range(1, C):
                source = lax.rem(me_c + (C - k), C)
                col_copy(
                    gcol, grecv_col.at[source], c_send_sem.at[k], c_recv_sem.at[k], me_c + k
                ).wait_recv()
            pending += copies
            gram = grecv_col[0]
            for c in range(1, C):
                gram = gram + grecv_col[c]
        else:
            for q in range(Y):
                if it == 0:
                    fetch(q)
                part[it, q] = project((1 - core) * Y + q)
                copy = col_copy(
                    part.at[it, q], half_recv.at[it, q], a_send_sem.at[it, q], a_recv_sem.at[it, q], partner
                )
                copy.start()
                pending.append(copy)
            for q in range(Y):
                if it == 0:
                    fetch(Y + q)
                value = project(core * Y + q)
                col_copy(
                    part.at[it, q], half_recv.at[it, q], a_send_sem.at[it, q], a_recv_sem.at[it, q], partner
                ).wait_recv()
                y_sum[it, q, me_y] = value + half_recv[it, q]
                for k in range(1, Y):
                    copy = col_copy(
                        y_sum.at[it, q, me_y], y_sum.at[it, q, me_y],
                        y_send_sem.at[it, q, k], y_recv_sem.at[it, q, k], y_peer(k),
                    )
                    copy.start()
                    pending.append(copy)
            gram = None
            for q in range(C):
                if q < Y:
                    c = core * Y + q
                    for k in range(1, Y):
                        source = lax.rem(me_y + (Y - k), Y)
                        col_copy(
                            y_sum.at[it, q, source], y_sum.at[it, q, source],
                            y_send_sem.at[it, q, k], y_recv_sem.at[it, q, k], y_peer(k),
                        ).wait_recv()
                    value = y_sum[it, q, 0]
                    for y in range(1, Y):
                        value = value + y_sum[it, q, y]
                    if it > 0:
                        value = value * inv_root
                    s_ref[it, c] = value
                    copy = col_copy(
                        s_ref.at[it, c], s_ref.at[it, c], s_send_sem.at[it, q], s_recv_sem.at[it, q], partner
                    )
                    copy.start()
                    pending.append(copy)
                else:
                    c = (1 - core) * Y + q - Y
                    col_copy(
                        s_ref.at[it, c], s_ref.at[it, c], s_send_sem.at[it, q - Y], s_recv_sem.at[it, q - Y], partner
                    ).wait_recv()
                    value = s_ref[it, c]
                high = value.astype(jnp.bfloat16)
                low = (value - high.astype(jnp.float32)).astype(jnp.bfloat16)
                lhs[:K, :] = high
                lhs[K:, :] = low
                if q < C - 1 or w % 128:
                    product = jnp.dot(lhs[...], slab[c], preferred_element_type=jnp.float32)
                    product = product[:K] + product[K:]
                    zacc[...] = product if q == 0 else zacc[...] + product
                gram_part[it, c] = square(value)
            gram = gram_part[it, 0]
            for c in range(1, C):
                gram = gram + gram_part[it, c]

        gsend_row[it] = gram
        for k in range(1, R):
            copy = row_copy(
                gsend_row.at[it], grecv_row.at[it, me_r], g_send_sem.at[it, k], g_recv_sem.at[it, k], k
            )
            copy.start()
            pending.append(copy)
        grecv_row[it, me_r] = gram

        if it < ITERS:
            last = (1 - core) * Y + Y - 1
            if w % 128:
                for r in range(R):
                    zpart[it, r] = zacc[:, r * w : (r + 1) * w]
            z_copies = []
            for k in list(range(1, R)) + [0]:
                r = row_peer(k)
                if w % 128 == 0:
                    span = pl.ds(pl.multiple_of(r * w, w), w)
                    product = jnp.dot(lhs[...], slab[last, :, span], preferred_element_type=jnp.float32)
                    zpart[it, r] = zacc[:, span] + product[:K] + product[K:]
                if k > 0:
                    copy = row_copy(
                        zpart.at[it, r], zrecv.at[it, k], z_send_sem.at[it, k], z_recv_sem.at[it, k], k
                    )
                    copy.start()
                    z_copies.append((k, copy))

        for k in range(1, R):
            row_copy(
                gsend_row.at[it], grecv_row.at[it, row_from(k)], g_send_sem.at[it, k], g_recv_sem.at[it, k], k
            ).wait_recv()
        gram = grecv_row[it, 0]
        for r in range(1, R):
            gram = gram + grecv_row[it, r]
        upper, inverse = factorize(gram)

        if it == ITERS:
            ortho = jnp.dot(inverse, own, precision=HIGHEST, preferred_element_type=jnp.float32)
            basis_ref[...] = ortho * scale
            factor_ref[...] = upper / scale
        else:
            total = zpart[it, me_r]
            for k, copy in z_copies:
                copy.wait_recv()
                total = total + zrecv[it, k]
                pending.append(copy)
            back[it, me_r] = jnp.dot(
                inverse, total, precision=HIGHEST, preferred_element_type=jnp.float32
            ).astype(jnp.bfloat16)
            for k in range(1, R):
                copy = row_copy(
                    back.at[it, me_r], back.at[it, me_r], b_send_sem.at[it, k], b_recv_sem.at[it, k], k
                )
                copy.start()
                pending.append(copy)
            for k in range(1, R):
                r = row_from(k)
                row_copy(
                    back.at[it, r], back.at[it, r], b_send_sem.at[it, k], b_recv_sem.at[it, k], k
                ).wait_recv()
            for r in range(R):
                x_ref[:, r * w : (r + 1) * w] = back[it, r]

    for copy in pending:
        copy.wait_send()


def body(affinity, seed_values, sku_ids):
    R, C = lax.axis_size("row"), lax.axis_size("col")
    K = seed_values.shape[0]
    rows, width = affinity.shape
    piece, w, Y = rows // C, width // R, C // 2
    dims = (R, C, K, piece, width, 1.0 / math.sqrt(width * C), math.sqrt(rows * R))
    f32, bf16 = jnp.float32, jnp.bfloat16
    dma = pltpu.SemaphoreType.DMA
    vmem = pl.BlockSpec(memory_space=pltpu.VMEM)
    return pl.pallas_call(
        functools.partial(kernel, dims),
        out_shape=(
            jax.ShapeDtypeStruct((K, piece), f32),
            jax.ShapeDtypeStruct((K, K), f32),
        ),
        in_specs=[
            pl.BlockSpec(memory_space=pl.ANY),
            pl.BlockSpec(memory_space=pltpu.SMEM),
            vmem,
        ],
        out_specs=(vmem, vmem),
        scratch_shapes=[
            pltpu.VMEM((C, piece, width), bf16),
            pltpu.VMEM((C, width, piece), bf16),
            pltpu.VMEM((K, width), bf16),
            pltpu.VMEM((ITERS, Y, K, piece), f32),
            pltpu.VMEM((ITERS, Y, K, piece), f32),
            pltpu.VMEM((ITERS, Y, Y, K, piece), f32),
            pltpu.VMEM((C, K, piece), f32),
            pltpu.VMEM((C, K, piece), f32),
            pltpu.VMEM((ITERS, C, K, piece), f32),
            pltpu.VMEM((2 * K, piece), bf16),
            pltpu.VMEM((K, width), f32),
            pltpu.VMEM((ITERS, R, K, w), f32),
            pltpu.VMEM((ITERS, R, K, w), f32),
            pltpu.VMEM((ITERS, R, K, w), bf16),
            pltpu.VMEM((ITERS + 1, K, K), f32),
            pltpu.VMEM((ITERS + 1, R, K, K), f32),
            pltpu.VMEM((C, K, K), f32),
            pltpu.VMEM((K, K), f32),
            pltpu.VMEM((ITERS, C, K, K), f32),
            dma((C,)),
            dma((ITERS, Y)), dma((ITERS, Y)),
            dma((ITERS, Y, Y)), dma((ITERS, Y, Y)),
            dma((C,)), dma((C,)),
            dma((ITERS, Y)), dma((ITERS, Y)),
            dma((ITERS, R)), dma((ITERS, R)),
            dma((ITERS, R)), dma((ITERS, R)),
            dma((ITERS + 1, R)), dma((ITERS + 1, R)),
            dma((C,)), dma((C,)),
        ],
        compiler_params=pltpu.CompilerParams(
            collective_id=0, has_side_effects=True, vmem_limit_bytes=60 * 1024 * 1024
        ),
    )(affinity, seed_values, sku_ids[None, :])


def solution(mesh):
    placed = (P("row", "col"), P(), P("col"))
    return jax.shard_map(
        body, mesh=mesh, in_specs=placed, out_specs=(P(None, ("row", "col")), P()), check_vma=False
    )
```

```python
import functools
import math

import jax
import jax.numpy as jnp
from jax import lax
from jax.experimental import pallas as pl
from jax.experimental.pallas import tpu as pltpu
from jax.sharding import PartitionSpec as P

ITERS = 2
SUB = 2
DEPTH = 3
HIGHEST = lax.Precision.HIGHEST
MESH = pl.DeviceIdType.MESH

mix_first = -2048144789
mix_second = -1028477387
golden = -1640531535
salt_value = 1540483477


def shifted(value, amount):
    return lax.shift_right_logical(value, jnp.full(value.shape, amount, jnp.int32))


def scramble(value):
    value = jnp.bitwise_xor(value, shifted(value, 16))
    value = value * jnp.int32(mix_first)
    value = jnp.bitwise_xor(value, shifted(value, 13))
    value = value * jnp.int32(mix_second)
    return jnp.bitwise_xor(value, shifted(value, 16))


def test_matrix(seeds, skus, total_columns):
    first = scramble(jnp.bitwise_xor(seeds, skus * jnp.int32(golden)))
    second = scramble(jnp.bitwise_xor(first, jnp.int32(salt_value)))
    uniform_a = (shifted(first, 9) + 1).astype(jnp.float32) / 8388608.0
    uniform_b = (shifted(second, 9) + 1).astype(jnp.float32) / 8388608.0
    gauss = jnp.sqrt(-2.0 * jnp.log(uniform_a)) * jnp.cos(6.283185307179586 * uniform_b)
    return (gauss / math.sqrt(total_columns)).astype(jnp.bfloat16)


def factorize(gram):
    count = gram.shape[0]
    rows = lax.broadcasted_iota(jnp.int32, (count, count), 0)
    cols = lax.broadcasted_iota(jnp.int32, (count, count), 1)
    left = gram
    right = (rows == cols).astype(jnp.float32)
    for j in range(count):
        pivot = left[j : j + 1, j : j + 1]
        inv = lax.rsqrt(pivot)
        inv = inv * (1.5 - 0.5 * (pivot * inv) * inv)
        left_row = left[j : j + 1, :] * inv
        right_row = right[j : j + 1, :] * inv
        factor = left[:, j : j + 1] * inv
        left = jnp.where(rows == j, left_row, jnp.where(rows > j, left - factor * left_row, left))
        right = jnp.where(rows == j, right_row, jnp.where(rows > j, right - factor * right_row, right))
    return jnp.where(rows <= cols, left, 0.0), right


def kernel(
    dims,
    slab_hbm, seed_ref, sku_ref,
    basis_ref, factor_ref,
    slab, slab_t, x_ref, part, half_recv, y_sum, part_last, recv_last, s_ref, lhs, zacc, zpart, zrecv, back,
    gsend_row, grecv_row, grecv_col, gcol, gram_part, mine,
    load_sem, a_send_sem, a_recv_sem, y_send_sem, y_recv_sem, last_send_sem, last_recv_sem, s_send_sem, s_recv_sem,
    z_send_sem, z_recv_sem, b_send_sem, b_recv_sem, g_send_sem, g_recv_sem, c_send_sem, c_recv_sem,
):
    R, C, K, piece, width, inv_root, scale = dims
    w = width // R
    me_r = lax.axis_index("row")
    me_c = lax.axis_index("col")

    Y = C // 2
    core, me_y = lax.rem(me_c, 2), me_c // 2
    partner = me_y * 2 + (1 - core)

    def y_peer(k):
        return lax.rem(me_y + k, Y) * 2 + core

    def col_peer_of(k):
        return (1 - core) * Y + k if k < Y else core * Y + k - Y

    def row_peer(k):
        return lax.rem(me_r + k, R)

    def row_from(k):
        return lax.rem(me_r + (R - k), R)

    span = piece // SUB
    n_load = C * SUB

    def load(i):
        start = col_peer_of(i // SUB) * piece + (i % SUB) * span
        return pltpu.make_async_copy(
            slab_hbm.at[pl.ds(pl.multiple_of(start, span), span), :],
            slab.at[i // SUB, pl.ds((i % SUB) * span, span), :],
            load_sem.at[i],
        )

    for i in range(min(DEPTH, n_load)):
        load(i).start()

    barrier = pltpu.get_barrier_semaphore()
    for k in range(1, R):
        pl.semaphore_signal(barrier, inc=1, device_id={"row": row_peer(k)}, device_id_type=MESH)
    for k in range(1, C):
        pl.semaphore_signal(barrier, inc=1, device_id={"col": lax.rem(me_c + k, C)}, device_id_type=MESH)

    index = lax.broadcasted_iota(jnp.int32, (K, width), 0)
    seeds = jnp.zeros((K, width), jnp.int32)
    for k in range(K):
        seeds = jnp.where(index == k, seed_ref[k], seeds)
    x_ref[...] = test_matrix(seeds, jnp.broadcast_to(sku_ref[...], (K, width)), width * C)

    pl.semaphore_wait(barrier, (R - 1) + (C - 1))

    pending = []

    def col_copy(src, dst, send, recv, target):
        return pltpu.make_async_remote_copy(
            src_ref=src, dst_ref=dst, send_sem=send, recv_sem=recv,
            device_id={"col": lax.rem(target, C)}, device_id_type=MESH,
        )

    def row_copy(src, dst, send, recv, k):
        return pltpu.make_async_remote_copy(
            src_ref=src, dst_ref=dst, send_sem=send, recv_sem=recv,
            device_id={"row": row_peer(k)}, device_id_type=MESH,
        )

    def project(k):
        return jnp.dot(x_ref[...], slab_t[k], preferred_element_type=jnp.float32)

    def position(c):
        half = c // Y
        same = 1 - (half + core - 2 * half * core)
        return lax.rem(c, Y) + Y * same

    def send_half(it, q):
        copy = col_copy(
            part.at[it, q], half_recv.at[it, q], a_send_sem.at[it, q], a_recv_sem.at[it, q], partner
        )
        copy.start()
        pending.append(copy)

    def send_y(it, q, value):
        col_copy(
            part.at[it, q], half_recv.at[it, q], a_send_sem.at[it, q], a_recv_sem.at[it, q], partner
        ).wait_recv()
        y_sum[it, q, me_y] = value + half_recv[it, q]
        for k in range(1, Y):
            copy = col_copy(
                y_sum.at[it, q, me_y], y_sum.at[it, q, me_y],
                y_send_sem.at[it, q, k], y_recv_sem.at[it, q, k], y_peer(k),
            )
            copy.start()
            pending.append(copy)

    def square(value):
        return lax.dot_general(
            value, value, (((1,), (1,)), ((), ())), precision=HIGHEST, preferred_element_type=jnp.float32
        )

    for it in range(ITERS + 1):
        if it == ITERS:
            copies = []
            for k in list(range(2, C)) + [1]:
                target = lax.rem(me_y + k // 2, Y) * 2 + (1 - core if k % 2 else core)
                part_last[k] = project(position(target))
                copy = col_copy(
                    part_last.at[k], recv_last.at[k], last_send_sem.at[k], last_recv_sem.at[k], target
                )
                copy.start()
                copies.append(copy)
            own = project(position(me_c))
            for k in [1] + list(range(2, C)):
                copies[(k - 2) % (C - 1)].wait_recv()
                own = own + recv_last[k]
            pending += copies
            own = own * inv_root
            gram = square(own)
            gcol[...] = gram
            copies = []
            for k in range(1, C):
                copy = col_copy(gcol, grecv_col.at[me_c], c_send_sem.at[k], c_recv_sem.at[k], me_c + k)
                copy.start()
                copies.append(copy)
            grecv_col[me_c] = gram
            for k in range(1, C):
                source = lax.rem(me_c + (C - k), C)
                col_copy(
                    gcol, grecv_col.at[source], c_send_sem.at[k], c_recv_sem.at[k], me_c + k
                ).wait_recv()
            pending += copies
            gram = grecv_col[0]
            for c in range(1, C):
                gram = gram + grecv_col[c]
        else:
            if it == 0:
                for i in range(n_load + 1):
                    if i < n_load:
                        load(i).wait()
                        if i + DEPTH < n_load:
                            load(i + DEPTH).start()
                        here = slice((i % SUB) * span, (i % SUB + 1) * span)
                        slab_t[i // SUB, :, here] = slab[i // SUB, here, :].T
                    if i > 0:
                        k, sub = (i - 1) // SUB, (i - 1) % SUB
                        here = slice(sub * span, (sub + 1) * span)
                        value = jnp.dot(x_ref[...], slab_t[k, :, here], preferred_element_type=jnp.float32)
                        if k < Y:
                            part[it, k, :, here] = value
                            if sub == SUB - 1:
                                send_half(it, k)
                        else:
                            mine[:, here] = value
                            if sub == SUB - 1:
                                send_y(it, k - Y, mine[...])
            else:
                for q in range(Y):
                    part[it, q] = project(q)
                    send_half(it, q)
                for q in range(Y):
                    send_y(it, q, project(Y + q))
            gram = None
            for q in range(C):
                at = Y + q if q < Y else q - Y
                if q < Y:
                    c = core * Y + q
                    for k in range(1, Y):
                        source = lax.rem(me_y + (Y - k), Y)
                        col_copy(
                            y_sum.at[it, q, source], y_sum.at[it, q, source],
                            y_send_sem.at[it, q, k], y_recv_sem.at[it, q, k], y_peer(k),
                        ).wait_recv()
                    value = y_sum[it, q, 0]
                    for y in range(1, Y):
                        value = value + y_sum[it, q, y]
                    if it > 0:
                        value = value * inv_root
                    s_ref[it, c] = value
                    copy = col_copy(
                        s_ref.at[it, c], s_ref.at[it, c], s_send_sem.at[it, q], s_recv_sem.at[it, q], partner
                    )
                    copy.start()
                    pending.append(copy)
                else:
                    c = (1 - core) * Y + q - Y
                    col_copy(
                        s_ref.at[it, c], s_ref.at[it, c], s_send_sem.at[it, q - Y], s_recv_sem.at[it, q - Y], partner
                    ).wait_recv()
                    value = s_ref[it, c]
                high = value.astype(jnp.bfloat16)
                low = (value - high.astype(jnp.float32)).astype(jnp.bfloat16)
                lhs[:K, :] = high
                lhs[K:, :] = low
                if q < C - 1 or w % 128:
                    product = jnp.dot(lhs[...], slab[at], preferred_element_type=jnp.float32)
                    product = product[:K] + product[K:]
                    zacc[...] = product if q == 0 else zacc[...] + product
                gram_part[it, c] = square(value)
            gram = gram_part[it, 0]
            for c in range(1, C):
                gram = gram + gram_part[it, c]

        gsend_row[it] = gram
        for k in range(1, R):
            copy = row_copy(
                gsend_row.at[it], grecv_row.at[it, me_r], g_send_sem.at[it, k], g_recv_sem.at[it, k], k
            )
            copy.start()
            pending.append(copy)
        grecv_row[it, me_r] = gram

        if it < ITERS:
            last = Y - 1
            if w % 128:
                for r in range(R):
                    zpart[it, r] = zacc[:, r * w : (r + 1) * w]
            z_copies = []
            for k in list(range(1, R)) + [0]:
                r = row_peer(k)
                if w % 128 == 0:
                    cols = pl.ds(pl.multiple_of(r * w, w), w)
                    product = jnp.dot(lhs[...], slab[last, :, cols], preferred_element_type=jnp.float32)
                    zpart[it, r] = zacc[:, cols] + product[:K] + product[K:]
                if k > 0:
                    copy = row_copy(
                        zpart.at[it, r], zrecv.at[it, k], z_send_sem.at[it, k], z_recv_sem.at[it, k], k
                    )
                    copy.start()
                    z_copies.append((k, copy))

        for k in range(1, R):
            row_copy(
                gsend_row.at[it], grecv_row.at[it, row_from(k)], g_send_sem.at[it, k], g_recv_sem.at[it, k], k
            ).wait_recv()
        gram = grecv_row[it, 0]
        for r in range(1, R):
            gram = gram + grecv_row[it, r]
        upper, inverse = factorize(gram)

        if it == ITERS:
            ortho = jnp.dot(inverse, own, precision=HIGHEST, preferred_element_type=jnp.float32)
            basis_ref[...] = ortho * scale
            factor_ref[...] = upper / scale
        else:
            total = zpart[it, me_r]
            for k, copy in z_copies:
                copy.wait_recv()
                total = total + zrecv[it, k]
                pending.append(copy)
            back[it, me_r] = jnp.dot(
                inverse, total, precision=HIGHEST, preferred_element_type=jnp.float32
            ).astype(jnp.bfloat16)
            for k in range(1, R):
                copy = row_copy(
                    back.at[it, me_r], back.at[it, me_r], b_send_sem.at[it, k], b_recv_sem.at[it, k], k
                )
                copy.start()
                pending.append(copy)
            for k in range(1, R):
                r = row_from(k)
                row_copy(
                    back.at[it, r], back.at[it, r], b_send_sem.at[it, k], b_recv_sem.at[it, k], k
                ).wait_recv()
            for r in range(R):
                x_ref[:, r * w : (r + 1) * w] = back[it, r]

    for copy in pending:
        copy.wait_send()


def body(affinity, seed_values, sku_ids):
    R, C = lax.axis_size("row"), lax.axis_size("col")
    K = seed_values.shape[0]
    rows, width = affinity.shape
    piece, w, Y = rows // C, width // R, C // 2
    dims = (R, C, K, piece, width, 1.0 / math.sqrt(width * C), math.sqrt(rows * R))
    f32, bf16 = jnp.float32, jnp.bfloat16
    dma = pltpu.SemaphoreType.DMA
    vmem = pl.BlockSpec(memory_space=pltpu.VMEM)
    return pl.pallas_call(
        functools.partial(kernel, dims),
        out_shape=(
            jax.ShapeDtypeStruct((K, piece), f32),
            jax.ShapeDtypeStruct((K, K), f32),
        ),
        in_specs=[
            pl.BlockSpec(memory_space=pl.ANY),
            pl.BlockSpec(memory_space=pltpu.SMEM),
            vmem,
        ],
        out_specs=(vmem, vmem),
        scratch_shapes=[
            pltpu.VMEM((C, piece, width), bf16),
            pltpu.VMEM((C, width, piece), bf16),
            pltpu.VMEM((K, width), bf16),
            pltpu.VMEM((ITERS, Y, K, piece), f32),
            pltpu.VMEM((ITERS, Y, K, piece), f32),
            pltpu.VMEM((ITERS, Y, Y, K, piece), f32),
            pltpu.VMEM((C, K, piece), f32),
            pltpu.VMEM((C, K, piece), f32),
            pltpu.VMEM((ITERS, C, K, piece), f32),
            pltpu.VMEM((2 * K, piece), bf16),
            pltpu.VMEM((K, width), f32),
            pltpu.VMEM((ITERS, R, K, w), f32),
            pltpu.VMEM((ITERS, R, K, w), f32),
            pltpu.VMEM((ITERS, R, K, w), bf16),
            pltpu.VMEM((ITERS + 1, K, K), f32),
            pltpu.VMEM((ITERS + 1, R, K, K), f32),
            pltpu.VMEM((C, K, K), f32),
            pltpu.VMEM((K, K), f32),
            pltpu.VMEM((ITERS, C, K, K), f32),
            pltpu.VMEM((K, piece), f32),
            dma((C * SUB,)),
            dma((ITERS, Y)), dma((ITERS, Y)),
            dma((ITERS, Y, Y)), dma((ITERS, Y, Y)),
            dma((C,)), dma((C,)),
            dma((ITERS, Y)), dma((ITERS, Y)),
            dma((ITERS, R)), dma((ITERS, R)),
            dma((ITERS, R)), dma((ITERS, R)),
            dma((ITERS + 1, R)), dma((ITERS + 1, R)),
            dma((C,)), dma((C,)),
        ],
        compiler_params=pltpu.CompilerParams(
            collective_id=0, has_side_effects=True, vmem_limit_bytes=60 * 1024 * 1024
        ),
    )(affinity, seed_values, sku_ids[None, :])


def solution(mesh):
    placed = (P("row", "col"), P(), P("col"))
    return jax.shard_map(
        body, mesh=mesh, in_specs=placed, out_specs=(P(None, ("row", "col")), P()), check_vma=False
    )
```
